32 devices in a mesh: dp: 4 (over x, core), tensor: 8 (over z, y).
Axes of the slice: x: 2, y: 2, z: 4, core: 2. Of those that a mesh axis runs over, the one named last changes fastest.
Arguments:
- hidden: bfloat16 [4, 1024, 2048], P('dp', 'tensor'), may hold values from -6 to 6
- query_nope: bfloat16 [4, 1024, 2048], P('dp', 'tensor'), may hold values from -6 to 6
- query_rope: bfloat16 [4, 1024, 1024], P('dp', 'tensor'), may hold values from -300 to 300
- segments: int32 [4, 1024], P('dp'), may hold values from 0 to 65, as said below
- w_kva: bfloat16 [2048, 576], replicated, may hold values from -0.125 to 0.125
- w_kb: bfloat16 [16, 512, 128], replicated, may hold values from -0.5 to 0.5
- w_vb: bfloat16 [16, 512, 128], replicated, may hold values from -0.25 to 0.25
- w_o: bfloat16 [2048, 2048], P('tensor'), may hold values from -0.125 to 0.125
- route_ids: int32 [4, 1024, 6], P('dp', 'tensor'), may hold values from 0 to 15, all different within a row; in each aligned block of 128 rows (0 to 127, 128 to 255, ..., all dimensions but the last counted through in order) at most 64 rows name the same one
- route_weights: float32 [4, 1024, 6], P('dp', 'tensor'), may hold values from 0.05 to 0.35
- w_in: bfloat16 [32, 2048, 1408], P(('dp', 'tensor')), may hold values from -0.125 to 0.125
- w_down: bfloat16 [32, 704, 2048], P(('dp', 'tensor')), may hold values from -0.15625 to 0.15625
- page_table: int32 [4, 8], P('dp'), may hold values from 0 to 7, each once within a row
Outputs:
- layer_out: bfloat16 [4, 1024, 2048], P('dp', 'tensor')
- pool_latent: bfloat16 [4, 8, 128, 512], P('dp', 'tensor')
- pool_rope: bfloat16 [4, 8, 128, 64], P('dp', 'tensor')
The draws below stay inside these ranges and needn't reach their ends.
Inputs may be any that keep to these rules, and one draw needn't show every extreme that they name: `segments`: in each stream ids start at 0, never fall and each segment is contiguous; the first segment has id 0, the last segment has id 65, the others are numbered 1, 2, ... in order; exactly one segment holds 512 tokens, the last may be cut short, every other holds 16 to 256. `route_ids`: in the rows of one device no expert is named more than 64 times, and that count is reached. `page_table`: each row is a permutation of the pool slots.
All inputs are finite; a program needn't handle non-finite values.
Results may differ from the reference program's by a relative error of at most 0.014.
Values may be sent and summed in bfloat16 or wider, within the bound.
A program may use at most 128 MiB of HBM per device.

```python
import math
import jax
import jax.numpy as jnp
import numpy as np
from jax import lax

D = 2048
HEADS = 16
HD = 128
RD = 64
LAT = 512
FF = 1408
TOP = 6
TOK_DEV = 128
PAGE = 128
EXPERTS = 16
TOK_STREAM = 1024
LONG = 512
SEG_MIN = 16
SEG_MAX = 256
CAP = 64
PAGES = 8
N_DP = 4


def draw_segments(key, part):

    def one_stream(stream_key):
        seg_count = TOK_STREAM // SEG_MIN + 2
        length_key, pick_key = jax.random.split(stream_key)
        lengths = jax.random.randint(length_key, (seg_count,), SEG_MIN, SEG_MAX + 1)
        chosen = jax.random.randint(pick_key, (), 0, 2)
        lengths = jnp.where(jnp.arange(seg_count) == chosen, LONG, lengths)
        ends = jnp.cumsum(lengths)
        positions = jnp.arange(TOK_STREAM)
        raw_ids = jnp.sum((ends[None, :] <= positions[:, None]).astype(jnp.int32), axis=1).astype(jnp.int32)
        last_raw = raw_ids[TOK_STREAM - 1]
        return jnp.where(raw_ids == last_raw, seg_count - 1, raw_ids).astype(jnp.int32)
    return jax.vmap(one_stream)(jax.random.split(jax.random.fold_in(key, 11), N_DP))


def draw_query_rope(key, part):
    shape = (N_DP, TOK_STREAM, HEADS * RD)
    base_key = jax.random.fold_in(jax.random.fold_in(key, 23), 0)
    return jnp.clip(jax.random.normal(base_key, shape, jnp.float32), -6.0, 6.0).astype(jnp.bfloat16)


def block_scale(rng, dims, pieces, least, high):
    gain = 1.0
    for position, blocks in pieces:
        draws = jax.random.uniform(jax.random.fold_in(jax.random.fold_in(rng, 6), position), (blocks,), jnp.float32, least / len(pieces), high / len(pieces))
        gain = gain * jnp.repeat(jnp.exp(draws), dims[position] // blocks).reshape((-1,) + (1,) * (len(dims) - 1 - position))
    return gain


def shared_out(key, own, number, rows, count, top, bound, skew):
    sequence = jax.random.permutation(key, count)
    crowded, ordinary = shares(count, rows * top, bound, skew, True), shares(count, rows * top, bound, skew, False)
    places = jnp.arange(count)

    def named(tallies, offset_by):
        used = int((tallies > 0).sum())
        fixed = max(1, used // 4)
        moved = fixed + (places - fixed + offset_by * (used - fixed)) % max(1, count - fixed)
        return jnp.zeros((count,), jnp.int32).at[sequence[jnp.where(places < fixed, places, moved)]].set(jnp.asarray(tallies, jnp.int32))

    tallies = jnp.where(number % 4 == 0, named(crowded, number // 4), named(ordinary, number - number // 4 - 1))
    mixed = jax.random.permutation(jax.random.fold_in(own, 3), count)
    source_of, sink = mixed[0:count // 2 * 2:2], mixed[1:count // 2 * 2:2]
    margin = jnp.minimum(tallies[source_of] - 1, bound - tallies[sink]) // 2
    margin = jnp.where((source_of == sequence[0]) | (sink == sequence[0]) | (tallies[sink] == 0), 0, jnp.maximum(margin, 0))
    moved = jax.random.randint(jax.random.fold_in(own, 4), (count // 2,), 0, 1 << 20) % (margin + 1)
    tallies = tallies.at[source_of].add(-moved).at[sink].add(moved)
    labels = jnp.searchsorted(jnp.cumsum(tallies), jnp.arange(rows * top), side="right").astype(jnp.int32)
    table = labels.reshape(top, rows).T
    table = table[jax.random.permutation(jax.random.fold_in(own, 1), rows)]
    offset_by = jax.random.randint(jax.random.fold_in(own, 2), (rows, 1), 0, top)
    return jnp.take_along_axis(table, (jnp.arange(top)[None, :] + offset_by) % top, axis=1)


def shares(count, total, reach, skew, full):
    loads = [(1 << 20) // math.isqrt(grade ** skew) + 1 for grade in range(1, count + 1)]
    largest = reach if full else min(reach, max(-(-total // count), total * loads[0] // sum(loads)))
    least = 1 if total - largest >= count - 1 else 0
    holding, surplus = [largest] + [least] * (count - 1), total - largest - least * (count - 1)
    while surplus > 0:
        movable = [i for i in range(1, count) if holding[i] < largest] or [i for i in range(1, count) if holding[i] < reach]
        pool, remaining = sum([loads[i] for i in movable]), surplus
        for i in movable:
            extra = min(reach - holding[i], max(1, remaining * loads[i] // pool), surplus)
            holding[i] = holding[i] + extra
            surplus = surplus - extra
    return np.array(holding)


def gaussian(rng, extent, scale, limit, shards=(), kind=jnp.bfloat16):
    values = jax.random.normal(rng, extent, jnp.float32) * scale
    if len(shards) > 0:
        values = block_scale(rng, extent, shards, -0.22, 0.18) * values
    return jnp.clip(values, min=-limit, max=limit).astype(kind)


def setup_inputs(seed: int = 0) -> dict:
    splits = jax.random.split(jax.random.key(seed), 14)
    hidden = gaussian(splits[0], (N_DP, TOK_STREAM, D), 1.0, 6.0, ((0, 4), (1, 8)))
    query_nope = gaussian(splits[1], (N_DP, TOK_STREAM, HEADS * HD), 1.0, 6.0, ((0, 4), (1, 8)))
    query_rope = draw_query_rope(jax.random.fold_in(splits[13], 71), 0)
    segments = draw_segments(jax.random.fold_in(splits[13], 71), 0)
    w_kva = gaussian(splits[4], (D, LAT + RD), D ** -0.5, 0.125)
    w_kb = gaussian(splits[5], (HEADS, LAT, HD), HD ** -0.5, 0.5)
    w_vb = gaussian(splits[6], (HEADS, LAT, HD), LAT ** -0.5, 0.25)
    w_o = gaussian(splits[7], (HEADS * HD, D), (HEADS * HD) ** -0.5, 0.125, ((0, 8),))
    route_ids_keys = jax.random.split(jax.random.fold_in(splits[8], 1), N_DP * TOK_STREAM // TOK_DEV)
    route_ids_turns = jax.random.permutation(jax.random.fold_in(splits[8], 3), N_DP * TOK_STREAM // TOK_DEV)
    route_ids = jax.vmap(lambda own, number: shared_out(jax.random.fold_in(splits[8], 2), own, number, TOK_DEV, EXPERTS, TOP, CAP, 2))(route_ids_keys, route_ids_turns).reshape((N_DP, TOK_STREAM, TOP))
    route_weights = jnp.clip(0.05 + 0.29999999 * jax.random.uniform(splits[9], (N_DP, TOK_STREAM, TOP), jnp.float32) ** block_scale(splits[9], (N_DP, TOK_STREAM, TOP), ((0, 4), (1, 8)), -0.2, 0.2), 0.05, 0.35)
    w_in = gaussian(splits[10], (2 * EXPERTS, D, FF), D ** -0.5, 0.125, ((0, 32),))
    w_down = gaussian(splits[11], (2 * EXPERTS, FF // 2, D), FF ** -0.5, 0.15625, ((0, 32),))
    page_table = jax.vmap(lambda own: jax.random.permutation(own, PAGES))(jax.random.split(splits[12], N_DP)).reshape((N_DP, PAGES)).astype(jnp.int32)
    return dict(hidden=hidden, query_nope=query_nope, query_rope=query_rope, segments=segments, w_kva=w_kva, w_kb=w_kb, w_vb=w_vb, w_o=w_o, route_ids=route_ids, route_weights=route_weights, w_in=w_in, w_down=w_down, page_table=page_table)


eps_norm = 1e-06
masked_score = -1e+30

def rms_rows(values):
    return values * lax.rsqrt(lax.optimization_barrier(jnp.mean(values * values, axis=-1, keepdims=True)) + eps_norm)

def rotate(values, positions):
    width = values.shape[-1]
    half_width = width // 2
    freqs = 10000.0 ** (-jnp.arange(half_width, dtype=jnp.float32) * 2.0 / width)
    angles = positions[..., None].astype(jnp.float32) * freqs
    cosine = jnp.cos(angles)
    sine = jnp.sin(angles)
    first_half = values[..., :half_width]
    second_half = values[..., half_width:]
    return jnp.concatenate([first_half * cosine - second_half * sine, first_half * sine + second_half * cosine], axis=-1)

def reference(hidden, query_nope, query_rope, segments, w_kva, w_kb, w_vb, w_o, route_ids, route_weights, w_in, w_down, page_table):
    scale = float(HD + RD) ** (-0.5)
    stream_len = TOK_STREAM
    qblock = min(512, stream_len)
    window = min(stream_len, qblock + LONG)
    resid_list = []
    normed_list = []
    pools_lat = []
    pools_rot = []
    for stream in range(N_DP):
        tokens = hidden[stream]
        kv_proj = jnp.dot(tokens, w_kva, preferred_element_type=jnp.float32)
        latent = rms_rows(kv_proj[:, :LAT]).astype(jnp.bfloat16)
        positions = jnp.arange(stream_len, dtype=jnp.int32)
        key_rope = rotate(kv_proj[:, LAT:], positions).astype(jnp.bfloat16)
        query_rot = rotate(query_rope[stream].astype(jnp.float32).reshape(stream_len, HEADS, RD), positions[:, None]).astype(jnp.bfloat16)
        query_lat = jnp.einsum('thd,hld->thl', query_nope[stream].astype(jnp.float32).reshape(stream_len, HEADS, HD), w_kb.astype(jnp.float32)).astype(jnp.bfloat16)
        seg_ids = segments[stream]

        def attend_block(block_no):
            q_first = block_no * qblock
            k_first = jnp.maximum(q_first + qblock - window, 0)
            q_lat = lax.dynamic_slice_in_dim(query_lat, q_first, qblock, 0).astype(jnp.float32)
            q_rot = lax.dynamic_slice_in_dim(query_rot, q_first, qblock, 0).astype(jnp.float32)
            k_lat = lax.dynamic_slice_in_dim(latent, k_first, window, 0).astype(jnp.float32)
            k_rot = lax.dynamic_slice_in_dim(key_rope, k_first, window, 0).astype(jnp.float32)
            q_seg = lax.dynamic_slice_in_dim(seg_ids, q_first, qblock, 0)
            k_seg = lax.dynamic_slice_in_dim(seg_ids, k_first, window, 0)
            scores = (jnp.einsum('qhl,kl->qhk', q_lat, k_lat) + jnp.einsum('qhr,kr->qhk', q_rot, k_rot)) * scale
            q_pos = q_first + jnp.arange(qblock, dtype=jnp.int32)
            k_pos = k_first + jnp.arange(window, dtype=jnp.int32)
            allowed = (q_seg[:, None] == k_seg[None, :]) & (k_pos[None, :] <= q_pos[:, None])
            scores = jnp.where(allowed[:, None, :], scores, masked_score)
            peak = lax.optimization_barrier(jnp.max(scores, axis=-1, keepdims=True))
            expo = jnp.exp(scores - peak)
            row_sum = lax.optimization_barrier(jnp.sum(expo, axis=-1))
            expw = expo.astype(jnp.bfloat16)
            mixed_lat = jnp.einsum('qhk,kl->qhl', expw.astype(jnp.float32), k_lat) / row_sum[..., None]
            return mixed_lat.astype(jnp.bfloat16)
        mixed_lat = lax.map(attend_block, jnp.arange(stream_len // qblock, dtype=jnp.int32)).reshape(stream_len, HEADS, LAT)
        heads_out = jnp.einsum('thl,hld->thd', mixed_lat.astype(jnp.float32), w_vb.astype(jnp.float32)).astype(jnp.bfloat16).reshape(stream_len, HEADS * HD)
        attn_out = jnp.dot(heads_out, w_o, preferred_element_type=jnp.float32)
        resid = (tokens.astype(jnp.float32) + attn_out).astype(jnp.bfloat16)
        normed = rms_rows(resid.astype(jnp.float32)).astype(jnp.bfloat16)
        resid_list.append(resid)
        normed_list.append(normed)
        pages_lat = latent.reshape(PAGES, PAGE, LAT)
        pages_rot = key_rope.reshape(PAGES, PAGE, RD)
        pools_lat.append(jnp.zeros_like(pages_lat).at[page_table[stream]].set(pages_lat))
        pools_rot.append(jnp.zeros_like(pages_rot).at[page_table[stream]].set(pages_rot))
    normed_all = jnp.concatenate(normed_list, axis=0)
    resid_all = jnp.concatenate(resid_list, axis=0)
    row_total = normed_all.shape[0]
    block_count = row_total // TOK_DEV
    expert_ids = route_ids.reshape(block_count, TOK_DEV * TOP)
    one_hot = (expert_ids[:, :, None] == jnp.arange(EXPERTS, dtype=jnp.int32)[None, None, :]).astype(jnp.int32)
    slot_in = lax.optimization_barrier(jnp.sum((jnp.cumsum(one_hot, axis=1) - 1) * one_hot, axis=2))
    block_no = jnp.arange(block_count, dtype=jnp.int32)[:, None]
    buffer_pos = (expert_ids * (block_count * CAP) + block_no * CAP + slot_in).reshape(-1).astype(jnp.int32)
    assign_total = row_total * TOP
    source = jnp.full((EXPERTS * block_count * CAP,), assign_total, jnp.int32)
    source = source.at[buffer_pos].set(jnp.arange(assign_total, dtype=jnp.int32)).reshape(EXPERTS, block_count * CAP)
    padded = jnp.concatenate([normed_all, jnp.zeros((1, D), jnp.bfloat16)], axis=0)
    weight_flat = jnp.concatenate([route_weights.reshape(-1), jnp.zeros((1,), jnp.float32)], axis=0)
    halves_in = w_in.reshape(EXPERTS, 2, D, FF)
    halves_out = w_down.reshape(EXPERTS, 2, FF // 2, D)

    def expert_step(combined, expert_item):
        src_rows, weights_in, weights_out = expert_item
        token_rows = src_rows // TOP
        rows_in = padded[token_rows]
        summed = jnp.zeros((rows_in.shape[0], D), jnp.float32)
        for half in range(2):
            gate_up = jnp.dot(rows_in, weights_in[half], preferred_element_type=jnp.float32)
            activated = (jax.nn.silu(gate_up[:, :FF // 2]) * gate_up[:, FF // 2:]).astype(jnp.bfloat16)
            part_out = lax.optimization_barrier(jnp.dot(activated, weights_out[half], preferred_element_type=jnp.float32).astype(jnp.bfloat16))
            summed = summed + part_out.astype(jnp.float32)
        combined = combined.at[token_rows].add(summed * weight_flat[src_rows][:, None])
        return (combined, None)
    combined, _ = lax.scan(expert_step, jnp.zeros((row_total + 1, D), jnp.float32), (source, halves_in, halves_out))
    layer_out = (resid_all.astype(jnp.float32) + combined[:row_total]).astype(jnp.bfloat16).reshape(N_DP, TOK_STREAM, D)
    return (layer_out, jnp.stack(pools_lat, axis=0), jnp.stack(pools_rot, axis=0))
```

```python
import jax
import jax.numpy as jnp
from jax import lax
from jax.experimental import pallas as pl
from jax.experimental.pallas import tpu as pltpu
from jax.sharding import PartitionSpec as P

MESH = pl.DeviceIdType.MESH

PAGE = 128


eps_norm = 1e-06
masked_score = -1e30


def rms_rows(values):
    return values * lax.rsqrt(jnp.mean(values * values, axis=-1, keepdims=True) + eps_norm)


def rotate(values, positions):
    width = values.shape[-1]
    half_width = width // 2
    freqs = 10000.0 ** (-jnp.arange(half_width, dtype=jnp.float32) * 2.0 / width)
    angles = positions[..., None].astype(jnp.float32) * freqs
    cosine = jnp.cos(angles)
    sine = jnp.sin(angles)
    first_half = values[..., :half_width]
    second_half = values[..., half_width:]
    return jnp.concatenate(
        [first_half * cosine - second_half * sine, first_half * sine + second_half * cosine],
        axis=-1,
    )


def attend(carry_in, queries, keys_lat, keys_rot, keys_seg, key_first):
    peak, row_sum, numerator = carry_in
    query_lat, query_rot, query_seg, positions, scale = queries
    scores = jnp.einsum("qhl,kl->qhk", query_lat, keys_lat, preferred_element_type=jnp.float32)
    scores = (
        scores + jnp.einsum("qhr,kr->qhk", query_rot, keys_rot, preferred_element_type=jnp.float32)
    ) * scale
    key_pos = key_first + jnp.arange(keys_lat.shape[0], dtype=jnp.int32)
    allowed = (query_seg[:, None] == keys_seg[None, :]) & (key_pos[None, :] <= positions[:, None])
    scores = jnp.where(allowed[:, None, :], scores, masked_score)
    new_peak = jnp.maximum(peak, jnp.max(scores, axis=-1))
    shrink = jnp.exp(peak - new_peak)
    expo = jnp.exp(scores - new_peak[..., None])
    row_sum = row_sum * shrink + jnp.sum(expo, axis=-1)
    numerator = numerator * shrink[..., None] + jnp.einsum(
        "qhk,kl->qhl", expo.astype(jnp.bfloat16), keys_lat, preferred_element_type=jnp.float32
    )
    return (new_peak, row_sum, numerator)


def expert_rows(received, gate_up_w, down_w):
    model_width = received.shape[-1]
    flat_rows = received.reshape(-1, model_width)
    gate_up = jnp.dot(flat_rows, gate_up_w, preferred_element_type=jnp.float32)
    half_units = down_w.shape[0]
    activated = (jax.nn.silu(gate_up[:, :half_units]) * gate_up[:, half_units:]).astype(
        jnp.bfloat16
    )
    return (
        jnp.dot(activated, down_w, preferred_element_type=jnp.float32)
        .astype(jnp.bfloat16)
        .reshape(received.shape)
    )


def place():
    dp = lax.axis_index("dp")
    member = lax.axis_index("tensor")
    return dp // 2, dp % 2, member // 2, member % 2


def device(x, core, z, y):
    return {"dp": x * 2 + core, "tensor": z * 2 + y}


def greet(partners):
    barrier = pltpu.get_barrier_semaphore()
    for partner in partners:
        pl.semaphore_signal(barrier, inc=1, device_id=partner, device_id_type=MESH)
    pl.semaphore_wait(barrier, len(partners))


def gather_kernel(depth, rows_ref, out_ref, own_sem, send_sem, recv_sem):
    x, core, z, y = place()
    half = rows_ref.shape[0] // 2
    sibling = device(x, 1 - core, z, y)
    over_y = device(x, core, z, 1 - y)
    over_x = device(1 - x, core, z, y)
    others = [lax.rem(z + step, depth) for step in range(1, depth)]
    over_z = [device(x, core, other, y) for other in others]
    started = []

    def slot(sx, sc, sz, sy):
        return (sx * 2 + sc) * (2 * depth) + sz * 2 + sy

    def send(block, part, target, own=False):
        span = pl.ds(part * half, half)
        copy = pltpu.make_async_remote_copy(
            src_ref=rows_ref.at[span] if own else out_ref.at[block, span],
            dst_ref=out_ref.at[block, span],
            send_sem=send_sem.at[len(started)],
            recv_sem=recv_sem.at[block, part],
            device_id=target,
            device_id_type=MESH,
        )
        copy.start()
        started.append(copy)

    def arrived(block, part):
        span = pl.ds(part * half, half)
        pltpu.make_async_remote_copy(
            src_ref=out_ref.at[block, span],
            dst_ref=out_ref.at[block, span],
            send_sem=send_sem.at[0],
            recv_sem=recv_sem.at[block, part],
            device_id=sibling,
            device_id_type=MESH,
        ).wait_recv()

    greet([sibling, over_y, over_x] + over_z)
    mine = slot(x, core, z, y)
    own = pltpu.make_async_copy(rows_ref, out_ref.at[mine], own_sem)
    own.start()
    near = (over_y, over_x)
    for part in range(2):
        for target in over_z:
            send(mine, part, target, True)
    for part in range(2):
        send(mine, part, near[part], True)
        send(mine, part, near[1 - part], True)
        send(mine, part, sibling, True)
    for step in range(1, depth):
        sz = lax.rem(z + depth - step, depth)
        for part in range(2):
            block = slot(x, core, sz, y)
            arrived(block, part)
            send(block, part, near[part])
            send(block, part, near[1 - part])
            send(block, part, sibling)
    for step in range(depth):
        sz = lax.rem(z + depth - step, depth)
        for part in range(2):
            block = slot(x, core, sz, 1 - y) if part == 0 else slot(1 - x, core, sz, y)
            arrived(block, part)
            send(block, part, near[1 - part])
            send(block, part, sibling)
    for far in range(2):
        for step in range(depth):
            sz = lax.rem(z + depth - step, depth)
            for part in range(2):
                if part == 0:
                    block = slot(1 - x, core, sz, (y + far) % 2)
                else:
                    block = slot((x + far) % 2, core, sz, 1 - y)
                arrived(block, part)
                send(block, part, sibling)
    for step in range(depth):
        sz = lax.rem(z + depth - step, depth)
        for sx in range(2):
            for sy in range(2):
                for part in range(2):
                    arrived(slot(sx, 1 - core, sz, sy), part)
    own.wait()
    for copy in started:
        copy.wait_send()


def gather_rows(rows, devices, depth):
    sends = 2 * (depth - 1 + depth + 2 * depth + 4 * depth)
    return pl.pallas_call(
        lambda *refs: gather_kernel(depth, *refs),
        name="gather_rows",
        out_shape=jax.ShapeDtypeStruct((devices,) + rows.shape, rows.dtype),
        in_specs=[pl.BlockSpec(memory_space=pl.ANY)],
        out_specs=pl.BlockSpec(memory_space=pl.ANY),
        scratch_shapes=[
            pltpu.SemaphoreType.DMA,
            pltpu.SemaphoreType.DMA((sends,)),
            pltpu.SemaphoreType.DMA((devices, 2)),
        ],
        compiler_params=pltpu.CompilerParams(collective_id=0, has_side_effects=True),
    )(rows)


def reduce_kernel(
    depth, part_ref, out_ref, first, second, third, fourth, send_sem, sem1, sem2, sem3, sem4
):
    x, core, z, y = place()
    half = out_ref.shape[0] // 2
    chunk = 16
    sibling = device(x, 1 - core, z, y)
    over_y = device(x, core, z, 1 - y)
    over_x = device(1 - x, core, z, y)
    others = [lax.rem(z + step, depth) for step in range(1, depth)]
    greet([sibling, over_y, over_x] + [device(x, core, other, y) for other in others])
    started = []

    def send(src, dst, recv_sem, target):
        copy = pltpu.make_async_remote_copy(
            src_ref=src,
            dst_ref=dst,
            send_sem=send_sem.at[len(started)],
            recv_sem=recv_sem,
            device_id=target,
            device_id_type=MESH,
        )
        copy.start()
        started.append(copy)

    def arrived(dst, recv_sem):
        pltpu.make_async_remote_copy(
            src_ref=dst,
            dst_ref=dst,
            send_sem=send_sem.at[0],
            recv_sem=recv_sem,
            device_id=sibling,
            device_id_type=MESH,
        ).wait_recv()

    def slot(dx, dc, dz, dy):
        return (dx * 2 + dc) * (2 * depth) + dz * 2 + dy

    def plane(dx, dz, dy):
        return (dx * 2 + dy) * depth + dz

    def span(part):
        return pl.ds(part * half, half)

    def add_into(target, part, sources):
        def body(step, carry):
            row = step * chunk
            rows = pl.ds(pl.multiple_of(part * half + row, chunk), chunk)
            short = pl.ds(pl.multiple_of(row, chunk), chunk)
            total = None
            for ref, index, whole in sources:
                value = ref[index, rows if whole else short, :].astype(jnp.float32)
                total = value if total is None else total + value
            if target is None:
                out_ref[rows, :] = total
            else:
                target[0][target[1], rows if target[2] else short, :] = total.astype(jnp.bfloat16)
            return carry

        lax.fori_loop(0, half // chunk, body, 0)

    def inner(part, near, dz):
        return (near * depth + dz) * 2 + part

    steps = [lax.rem(z + step, depth) for step in list(range(1, depth)) + [0]]

    def dest(part, far_first, far_second):
        if part == 0:
            return (x + far_first) % 2, (y + far_second) % 2
        return (x + far_second) % 2, (y + far_first) % 2

    order = [(1, 1), (1, 0), (0, 1), (0, 0)]
    for far_first, far_second in order:
        for dz in steps:
            for part in range(2):
                dx, dy = dest(part, far_first, far_second)
                index = plane(dx, dz, dy)
                send(
                    part_ref.at[slot(dx, 1 - core, dz, dy), span(part)],
                    first.at[index, span(part)],
                    sem1.at[index, part],
                    sibling,
                )
    for far_second in (1, 0):
        for dz in steps:
            for part in range(2):
                dx, dy = dest(part, 1, far_second)
                index = plane(dx, dz, dy)
                arrived(first.at[index, span(part)], sem1.at[index, part])
                add_into(
                    (first, index, True),
                    part,
                    [(part_ref, slot(dx, core, dz, dy), True), (first, index, True)],
                )
                there = inner(part, far_second, dz)
                send(
                    first.at[index, span(part)],
                    second.at[there],
                    sem2.at[there],
                    over_x if part == 0 else over_y,
                )
    for dz in steps:
        for part in range(2):
            dx, dy = dest(part, 0, 1)
            index = plane(dx, dz, dy)
            there = inner(part, 1, dz)
            arrived(first.at[index, span(part)], sem1.at[index, part])
            arrived(second.at[there], sem2.at[there])
            add_into(
                (second, there, False),
                part,
                [
                    (part_ref, slot(dx, core, dz, dy), True),
                    (first, index, True),
                    (second, there, False),
                ],
            )
            last = dz * 2 + part
            send(
                second.at[there],
                third.at[last],
                sem3.at[last],
                over_y if part == 0 else over_x,
            )
    for number, dz in enumerate(steps):
        for part in range(2):
            index = plane(x, dz, y)
            there = inner(part, 0, dz)
            last = dz * 2 + part
            arrived(first.at[index, span(part)], sem1.at[index, part])
            arrived(second.at[there], sem2.at[there])
            arrived(third.at[last], sem3.at[last])
            sources = [
                (part_ref, slot(x, core, dz, y), True),
                (first, index, True),
                (second, there, False),
                (third, last, False),
            ]
            if number < depth - 1:
                add_into((third, last, False), part, sources)
                end = number * 2 + part
                send(third.at[last], fourth.at[end], sem4.at[end], device(x, core, dz, y))
            else:
                for other in range(depth - 1):
                    end = other * 2 + part
                    arrived(fourth.at[end], sem4.at[end])
                    sources.append((fourth, end, False))
                add_into(None, part, sources)
    for copy in started:
        copy.wait_send()


def reduce_rows(parts, depth):
    devices, rows, width = parts.shape
    half = rows // 2
    sends = 8 * depth + 4 * depth + 2 * depth + 2 * (depth - 1)
    return pl.pallas_call(
        lambda *refs: reduce_kernel(depth, *refs),
        name="reduce_rows",
        out_shape=jax.ShapeDtypeStruct((rows, width), jnp.float32),
        in_specs=[pl.BlockSpec(memory_space=pltpu.VMEM)],
        out_specs=pl.BlockSpec(memory_space=pltpu.VMEM),
        scratch_shapes=[
            pltpu.VMEM((devices // 2, rows, width), jnp.bfloat16),
            pltpu.VMEM((4 * depth, half, width), jnp.bfloat16),
            pltpu.VMEM((2 * depth, half, width), jnp.bfloat16),
            pltpu.VMEM((2 * (depth - 1), half, width), jnp.bfloat16),
            pltpu.SemaphoreType.DMA((sends,)),
            pltpu.SemaphoreType.DMA((devices // 2, 2)),
            pltpu.SemaphoreType.DMA((4 * depth,)),
            pltpu.SemaphoreType.DMA((2 * depth,)),
            pltpu.SemaphoreType.DMA((2 * (depth - 1),)),
        ],
        compiler_params=pltpu.CompilerParams(
            collective_id=1, has_side_effects=True, vmem_limit_bytes=48 * 1024 * 1024
        ),
    )(parts)


def dense_experts(normed, gate_up_w, down_w, experts, capacity, all_share):
    devices = lax.axis_size("dp") * lax.axis_size("tensor")
    depth = lax.axis_size("tensor") // 2
    local_rows, model_width = normed.shape
    expert = (lax.axis_index("dp") * lax.axis_size("tensor") + lax.axis_index("tensor")) // 2
    chosen = jnp.arange(experts, dtype=jnp.int32) == expert
    share = jnp.sum(jnp.where(chosen, all_share, 0.0), axis=-1).reshape(devices, local_rows)
    named = share != 0.0
    order = jnp.arange(local_rows, dtype=jnp.int32)
    upper = (order[:, None] <= order[None, :]).astype(jnp.bfloat16)
    rank = jnp.dot(named.astype(jnp.bfloat16), upper, preferred_element_type=jnp.float32) - 1.0
    slots = jnp.arange(capacity, dtype=jnp.int32)
    pick = named[:, None, :] & (rank.astype(jnp.int32)[:, None, :] == slots[None, :, None])
    slot_share = jnp.sum(jnp.where(pick, share[:, None, :], 0.0), axis=-1).reshape(-1, 1)
    pick = pick.astype(jnp.bfloat16)
    everyone = gather_rows(normed, devices, depth)
    rows = jnp.einsum("sct,std->scd", pick, everyone, preferred_element_type=jnp.float32)
    rows = rows.astype(jnp.bfloat16).reshape(devices * capacity, model_width)
    gate_up = jnp.dot(rows, gate_up_w, preferred_element_type=jnp.float32)
    half_units = down_w.shape[0]
    activated = (jax.nn.silu(gate_up[:, :half_units]) * gate_up[:, half_units:]).astype(
        jnp.bfloat16
    )
    scaled = (jnp.dot(activated, down_w, preferred_element_type=jnp.float32) * slot_share).astype(
        jnp.bfloat16
    )
    scaled = scaled.reshape(devices, capacity, model_width)
    parts = jnp.einsum("sct,scd->std", pick, scaled, preferred_element_type=jnp.float32)
    return reduce_rows(parts.astype(jnp.bfloat16), depth)


def on_device(
    hidden,
    query_nope,
    query_rope,
    segments,
    w_kva,
    w_kb,
    w_vb,
    w_o,
    route_ids,
    route_weights,
    w_in,
    w_down,
    page_table,
):
    groups = lax.axis_size("tensor")
    stream_groups = lax.axis_size("dp")
    member = lax.axis_index("tensor")
    tokens = hidden[0]
    local_rows = tokens.shape[0]
    model_width = tokens.shape[1]
    stream_len = segments.shape[1]
    n_heads, lat_width, head_width = w_kb.shape
    rope_width = w_kva.shape[1] - lat_width
    top_count = route_ids.shape[2]
    scale = float(head_width + rope_width) ** (-0.5)
    kv_proj = jnp.dot(tokens, w_kva, preferred_element_type=jnp.float32)
    latent = rms_rows(kv_proj[:, :lat_width]).astype(jnp.bfloat16)
    first_row = member * local_rows
    positions = first_row + jnp.arange(local_rows, dtype=jnp.int32)
    key_rope = rotate(kv_proj[:, lat_width:], positions).astype(jnp.bfloat16)
    query_rot = rotate(
        query_rope[0].astype(jnp.float32).reshape(local_rows, n_heads, rope_width),
        positions[:, None],
    ).astype(jnp.bfloat16)
    query_lat = jnp.einsum(
        "thd,hld->thl",
        query_nope[0].reshape(local_rows, n_heads, head_width),
        w_kb,
        preferred_element_type=jnp.float32,
    ).astype(jnp.bfloat16)
    seg_all = segments[0]
    query_seg = lax.dynamic_slice_in_dim(seg_all, first_row, local_rows, 0)
    key_low = jnp.sum((seg_all < query_seg[0]).astype(jnp.int32))
    key_high = first_row + local_rows
    queries = (query_lat, query_rot, query_seg, positions, scale)
    start_state = (
        jnp.full((local_rows, n_heads), masked_score, jnp.float32),
        jnp.zeros((local_rows, n_heads), jnp.float32),
        jnp.zeros((local_rows, n_heads, lat_width), jnp.float32),
    )
    pages_dev = local_rows // PAGE
    page_row = page_table[0]
    slot_ids = member * pages_dev + jnp.arange(pages_dev, dtype=jnp.int32)
    page_of = jnp.sum(
        jnp.where(
            page_row[None, :] == slot_ids[:, None],
            jnp.arange(page_row.shape[0], dtype=jnp.int32)[None, :],
            0,
        ),
        axis=1,
    )
    page_rows = page_of[:, None] * PAGE + jnp.arange(PAGE, dtype=jnp.int32)[None, :]
    all_keys = lax.all_gather(
        jnp.concatenate([latent, key_rope], axis=1), "tensor", axis=0, tiled=True
    )
    all_latent, all_rope = all_keys[:, :lat_width], all_keys[:, lat_width:]
    experts = stream_groups * groups // 2
    capacity = max(2, min(local_rows, local_rows * top_count * 4 // (3 * experts)))
    dense = stream_groups * groups * local_rows <= 4 * experts * capacity
    if dense:
        one_hot = route_ids[0][:, :, None] == jnp.arange(experts, dtype=jnp.int32)
        share = jnp.sum(jnp.where(one_hot, route_weights[0][:, :, None], 0.0), axis=1)
        all_share = lax.all_gather(share, ("dp", "tensor"), axis=0, tiled=True)
    core = lax.axis_index("dp") % 2
    half_width = model_width // 2
    my_columns = lax.all_gather(
        lax.dynamic_slice_in_dim(w_o, core * half_width, half_width, 1),
        "tensor",
        axis=0,
        tiled=True,
    )
    its_columns = lax.ppermute(
        my_columns, "dp", [(number, number ^ 1) for number in range(stream_groups)]
    )
    key_block = min(512, stream_len)
    block_first = key_low // key_block
    block_end = (key_high + key_block - 1) // key_block

    def key_step(block_no, carry_in):
        key_first = block_no * key_block
        keys_lat = lax.dynamic_slice_in_dim(all_latent, key_first, key_block, 0)
        keys_rot = lax.dynamic_slice_in_dim(all_rope, key_first, key_block, 0)
        keys_seg = lax.dynamic_slice_in_dim(seg_all, key_first, key_block, 0)
        return attend(carry_in, queries, keys_lat, keys_rot, keys_seg, key_first)

    final_state = lax.fori_loop(block_first, block_end, key_step, start_state)
    pool_lat = all_latent[page_rows]
    pool_rot = all_rope[page_rows]
    mixed_lat = (final_state[2] / final_state[1][..., None]).astype(jnp.bfloat16)
    heads_out = (
        jnp.einsum("thl,hld->thd", mixed_lat, w_vb, preferred_element_type=jnp.float32)
        .astype(jnp.bfloat16)
        .reshape(local_rows, n_heads * head_width)
    )
    my_out = jnp.dot(heads_out, my_columns, preferred_element_type=jnp.float32)
    its_out = jnp.dot(heads_out, its_columns, preferred_element_type=jnp.float32)
    attn_out = jnp.where(
        core == 0,
        jnp.concatenate([my_out, its_out], axis=1),
        jnp.concatenate([its_out, my_out], axis=1),
    )
    resid = (tokens.astype(jnp.float32) + attn_out).astype(jnp.bfloat16)
    normed = rms_rows(resid.astype(jnp.float32)).astype(jnp.bfloat16)
    if dense:
        moe_out = dense_experts(
            normed,
            w_in[0],
            w_down[0],
            experts,
            capacity,
            all_share,
        )
        layer_out = (resid.astype(jnp.float32) + moe_out).astype(jnp.bfloat16)
        return (layer_out[None], pool_lat[None], pool_rot[None])
    expert_ids = route_ids[0].reshape(-1)
    assign_total = local_rows * top_count
    one_hot = (expert_ids[:, None] == jnp.arange(experts, dtype=jnp.int32)[None, :]).astype(
        jnp.int32
    )
    slot_in = jnp.sum((jnp.cumsum(one_hot, axis=0) - 1) * one_hot, axis=1)
    buffer_pos = expert_ids * capacity + slot_in
    source = (
        jnp.full((experts * capacity,), assign_total, jnp.int32)
        .at[buffer_pos]
        .set(jnp.arange(assign_total, dtype=jnp.int32))
    )
    padded = jnp.concatenate([normed, jnp.zeros((1, model_width), jnp.bfloat16)], axis=0)
    gathered_rows = padded[source // top_count]
    sending = gathered_rows.reshape(experts, 1, capacity, model_width)
    sending = jnp.broadcast_to(sending, (experts, 2, capacity, model_width)).reshape(
        2 * experts, capacity, model_width
    )
    returned = lax.all_to_all(
        expert_rows(
            lax.all_to_all(sending, ("dp", "tensor"), split_axis=0, concat_axis=0, tiled=True),
            w_in[0],
            w_down[0],
        ),
        ("dp", "tensor"),
        split_axis=0,
        concat_axis=0,
        tiled=True,
    )
    pairs = returned.reshape(experts, 2, capacity, model_width)
    merged = (pairs[:, 0].astype(jnp.float32) + pairs[:, 1].astype(jnp.float32)).reshape(
        experts * capacity, model_width
    )
    picked = merged[buffer_pos]
    weight_flat = route_weights[0].reshape(-1)
    moe_out = jnp.sum(
        (picked * weight_flat[:, None]).reshape(local_rows, top_count, model_width), axis=1
    )
    layer_out = (resid.astype(jnp.float32) + moe_out).astype(jnp.bfloat16)
    return (layer_out[None], pool_lat[None], pool_rot[None])


def solution(mesh):
    return jax.shard_map(
        on_device,
        mesh=mesh,
        in_specs=(
            P("dp", "tensor", None),
            P("dp", "tensor", None),
            P("dp", "tensor", None),
            P("dp", None),
            P(),
            P(),
            P(),
            P("tensor", None),
            P("dp", "tensor", None),
            P("dp", "tensor", None),
            P(("dp", "tensor"), None, None),
            P(("dp", "tensor"), None, None),
            P("dp", None),
        ),
        out_specs=(
            P("dp", "tensor", None),
            P("dp", "tensor", None, None),
            P("dp", "tensor", None, None),
        ),
        check_vma=False,
    )
```

```python
import jax
import jax.numpy as jnp
from jax import lax
from jax.experimental import pallas as pl
from jax.experimental.pallas import tpu as pltpu
from jax.sharding import PartitionSpec as P

MESH = pl.DeviceIdType.MESH

PAGE = 128


eps_norm = 1e-06
masked_score = -1e30


def rms_rows(values):
    return values * lax.rsqrt(jnp.mean(values * values, axis=-1, keepdims=True) + eps_norm)


def rotate(values, positions):
    width = values.shape[-1]
    half_width = width // 2
    freqs = 10000.0 ** (-jnp.arange(half_width, dtype=jnp.float32) * 2.0 / width)
    angles = positions[..., None].astype(jnp.float32) * freqs
    cosine = jnp.cos(angles)
    sine = jnp.sin(angles)
    first_half = values[..., :half_width]
    second_half = values[..., half_width:]
    return jnp.concatenate(
        [first_half * cosine - second_half * sine, first_half * sine + second_half * cosine],
        axis=-1,
    )


def attend(carry_in, queries, keys_lat, keys_rot, keys_seg, key_first):
    peak, row_sum, numerator = carry_in
    query_lat, query_rot, query_seg, positions, scale = queries
    scores = jnp.einsum("qhl,kl->qhk", query_lat, keys_lat, preferred_element_type=jnp.float32)
    scores = (
        scores + jnp.einsum("qhr,kr->qhk", query_rot, keys_rot, preferred_element_type=jnp.float32)
    ) * scale
    key_pos = key_first + jnp.arange(keys_lat.shape[0], dtype=jnp.int32)
    allowed = (query_seg[:, None] == keys_seg[None, :]) & (key_pos[None, :] <= positions[:, None])
    scores = jnp.where(allowed[:, None, :], scores, masked_score)
    new_peak = jnp.maximum(peak, jnp.max(scores, axis=-1))
    shrink = jnp.exp(peak - new_peak)
    expo = jnp.exp(scores - new_peak[..., None])
    row_sum = row_sum * shrink + jnp.sum(expo, axis=-1)
    numerator = numerator * shrink[..., None] + jnp.einsum(
        "qhk,kl->qhl", expo.astype(jnp.bfloat16), keys_lat, preferred_element_type=jnp.float32
    )
    return (new_peak, row_sum, numerator)


def expert_rows(received, gate_up_w, down_w):
    model_width = received.shape[-1]
    flat_rows = received.reshape(-1, model_width)
    gate_up = jnp.dot(flat_rows, gate_up_w, preferred_element_type=jnp.float32)
    half_units = down_w.shape[0]
    activated = (jax.nn.silu(gate_up[:, :half_units]) * gate_up[:, half_units:]).astype(
        jnp.bfloat16
    )
    return (
        jnp.dot(activated, down_w, preferred_element_type=jnp.float32)
        .astype(jnp.bfloat16)
        .reshape(received.shape)
    )


def place():
    dp = lax.axis_index("dp")
    member = lax.axis_index("tensor")
    return dp // 2, dp % 2, member // 2, member % 2


def device(x, core, z, y):
    return {"dp": x * 2 + core, "tensor": z * 2 + y}


def greet(partners):
    barrier = pltpu.get_barrier_semaphore()
    for partner in partners:
        pl.semaphore_signal(barrier, inc=1, device_id=partner, device_id_type=MESH)
    pl.semaphore_wait(barrier, len(partners))


def gather_kernel(depth, rows_ref, out_ref, own_sem, send_sem, recv_sem):
    x, core, z, y = place()
    half = rows_ref.shape[0] // 2
    sibling = device(x, 1 - core, z, y)
    over_y = device(x, core, z, 1 - y)
    over_x = device(1 - x, core, z, y)
    others = [lax.rem(z + step, depth) for step in range(1, depth)]
    over_z = [device(x, core, other, y) for other in others]
    started = []

    def slot(sx, sc, sz, sy):
        return (sx * 2 + sc) * (2 * depth) + sz * 2 + sy

    def send(block, part, target, own=False):
        span = pl.ds(part * half, half)
        copy = pltpu.make_async_remote_copy(
            src_ref=rows_ref.at[span] if own else out_ref.at[block, span],
            dst_ref=out_ref.at[block, span],
            send_sem=send_sem.at[len(started)],
            recv_sem=recv_sem.at[block, part],
            device_id=target,
            device_id_type=MESH,
        )
        copy.start()
        started.append(copy)

    def arrived(block, part):
        span = pl.ds(part * half, half)
        pltpu.make_async_remote_copy(
            src_ref=out_ref.at[block, span],
            dst_ref=out_ref.at[block, span],
            send_sem=send_sem.at[0],
            recv_sem=recv_sem.at[block, part],
            device_id=sibling,
            device_id_type=MESH,
        ).wait_recv()

    greet([sibling, over_y, over_x] + over_z)
    mine = slot(x, core, z, y)
    own = pltpu.make_async_copy(rows_ref, out_ref.at[mine], own_sem)
    own.start()
    near = (over_y, over_x)
    for part in range(2):
        for target in over_z:
            send(mine, part, target, True)
    for part in range(2):
        send(mine, part, near[part], True)
        send(mine, part, near[1 - part], True)
        send(mine, part, sibling, True)
    for step in range(1, depth):
        sz = lax.rem(z + depth - step, depth)
        for part in range(2):
            block = slot(x, core, sz, y)
            arrived(block, part)
            send(block, part, near[part])
            send(block, part, near[1 - part])
            send(block, part, sibling)
    for step in range(depth):
        sz = lax.rem(z + depth - step, depth)
        for part in range(2):
            block = slot(x, core, sz, 1 - y) if part == 0 else slot(1 - x, core, sz, y)
            arrived(block, part)
            send(block, part, near[1 - part])
            send(block, part, sibling)
    for far in range(2):
        for step in range(depth):
            sz = lax.rem(z + depth - step, depth)
            for part in range(2):
                if part == 0:
                    block = slot(1 - x, core, sz, (y + far) % 2)
                else:
                    block = slot((x + far) % 2, core, sz, 1 - y)
                arrived(block, part)
                send(block, part, sibling)
    for step in range(depth):
        sz = lax.rem(z + depth - step, depth)
        for sx in range(2):
            for sy in range(2):
                for part in range(2):
                    arrived(slot(sx, 1 - core, sz, sy), part)
    own.wait()
    for copy in started:
        copy.wait_send()


def gather_rows(rows, devices, depth):
    sends = 2 * (depth - 1 + depth + 2 * depth + 4 * depth)
    return pl.pallas_call(
        lambda *refs: gather_kernel(depth, *refs),
        name="gather_rows",
        out_shape=jax.ShapeDtypeStruct((devices,) + rows.shape, rows.dtype),
        in_specs=[pl.BlockSpec(memory_space=pl.ANY)],
        out_specs=pl.BlockSpec(memory_space=pl.ANY),
        scratch_shapes=[
            pltpu.SemaphoreType.DMA,
            pltpu.SemaphoreType.DMA((sends,)),
            pltpu.SemaphoreType.DMA((devices, 2)),
        ],
        compiler_params=pltpu.CompilerParams(collective_id=0, has_side_effects=True),
    )(rows)


def reduce_kernel(
    depth, part_ref, out_ref, first, second, third, fourth, send_sem, sem1, sem2, sem3, sem4
):
    x, core, z, y = place()
    half = out_ref.shape[0] // 2
    chunk = 16
    sibling = device(x, 1 - core, z, y)
    over_y = device(x, core, z, 1 - y)
    over_x = device(1 - x, core, z, y)
    others = [lax.rem(z + step, depth) for step in range(1, depth)]
    greet([sibling, over_y, over_x] + [device(x, core, other, y) for other in others])
    started = []

    def send(src, dst, recv_sem, target):
        copy = pltpu.make_async_remote_copy(
            src_ref=src,
            dst_ref=dst,
            send_sem=send_sem.at[len(started)],
            recv_sem=recv_sem,
            device_id=target,
            device_id_type=MESH,
        )
        copy.start()
        started.append(copy)

    def arrived(dst, recv_sem):
        pltpu.make_async_remote_copy(
            src_ref=dst,
            dst_ref=dst,
            send_sem=send_sem.at[0],
            recv_sem=recv_sem,
            device_id=sibling,
            device_id_type=MESH,
        ).wait_recv()

    def slot(dx, dc, dz, dy):
        return (dx * 2 + dc) * (2 * depth) + dz * 2 + dy

    def plane(dx, dz, dy):
        return (dx * 2 + dy) * depth + dz

    def span(part):
        return pl.ds(part * half, half)

    def add_into(target, part, sources):
        def body(step, carry):
            row = step * chunk
            rows = pl.ds(pl.multiple_of(part * half + row, chunk), chunk)
            short = pl.ds(pl.multiple_of(row, chunk), chunk)
            total = None
            for ref, index, whole in sources:
                value = ref[index, rows if whole else short, :].astype(jnp.float32)
                total = value if total is None else total + value
            if target is None:
                out_ref[rows, :] = total
            else:
                target[0][target[1], rows if target[2] else short, :] = total.astype(jnp.bfloat16)
            return carry

        lax.fori_loop(0, half // chunk, body, 0)

    def inner(part, near, dz):
        return (near * depth + dz) * 2 + part

    steps = [lax.rem(z + step, depth) for step in list(range(1, depth)) + [0]]

    def dest(part, far_first, far_second):
        if part == 0:
            return (x + far_first) % 2, (y + far_second) % 2
        return (x + far_second) % 2, (y + far_first) % 2

    order = [(1, 1), (1, 0), (0, 1), (0, 0)]
    for far_first, far_second in order:
        for dz in steps:
            for part in range(2):
                dx, dy = dest(part, far_first, far_second)
                index = plane(dx, dz, dy)
                send(
                    part_ref.at[slot(dx, 1 - core, dz, dy), span(part)],
                    first.at[index, span(part)],
                    sem1.at[index, part],
                    sibling,
                )
    for far_second in (1, 0):
        for dz in steps:
            for part in range(2):
                dx, dy = dest(part, 1, far_second)
                index = plane(dx, dz, dy)
                arrived(first.at[index, span(part)], sem1.at[index, part])
                add_into(
                    (first, index, True),
                    part,
                    [(part_ref, slot(dx, core, dz, dy), True), (first, index, True)],
                )
                there = inner(part, far_second, dz)
                send(
                    first.at[index, span(part)],
                    second.at[there],
                    sem2.at[there],
                    over_x if part == 0 else over_y,
                )
    for dz in steps:
        for part in range(2):
            dx, dy = dest(part, 0, 1)
            index = plane(dx, dz, dy)
            there = inner(part, 1, dz)
            arrived(first.at[index, span(part)], sem1.at[index, part])
            arrived(second.at[there], sem2.at[there])
            add_into(
                (second, there, False),
                part,
                [
                    (part_ref, slot(dx, core, dz, dy), True),
                    (first, index, True),
                    (second, there, False),
                ],
            )
            last = dz * 2 + part
            send(
                second.at[there],
                third.at[last],
                sem3.at[last],
                over_y if part == 0 else over_x,
            )
    for number, dz in enumerate(steps):
        for part in range(2):
            index = plane(x, dz, y)
            there = inner(part, 0, dz)
            last = dz * 2 + part
            arrived(first.at[index, span(part)], sem1.at[index, part])
            arrived(second.at[there], sem2.at[there])
            arrived(third.at[last], sem3.at[last])
            sources = [
                (part_ref, slot(x, core, dz, y), True),
                (first, index, True),
                (second, there, False),
                (third, last, False),
            ]
            if number < depth - 1:
                add_into((third, last, False), part, sources)
                end = number * 2 + part
                send(third.at[last], fourth.at[end], sem4.at[end], device(x, core, dz, y))
            else:
                for other in range(depth - 1):
                    end = other * 2 + part
                    arrived(fourth.at[end], sem4.at[end])
                    sources.append((fourth, end, False))
                add_into(None, part, sources)
    for copy in started:
        copy.wait_send()


def reduce_rows(parts, depth):
    devices, rows, width = parts.shape
    half = rows // 2
    sends = 8 * depth + 4 * depth + 2 * depth + 2 * (depth - 1)
    return pl.pallas_call(
        lambda *refs: reduce_kernel(depth, *refs),
        name="reduce_rows",
        out_shape=jax.ShapeDtypeStruct((rows, width), jnp.float32),
        in_specs=[pl.BlockSpec(memory_space=pltpu.VMEM)],
        out_specs=pl.BlockSpec(memory_space=pltpu.VMEM),
        scratch_shapes=[
            pltpu.VMEM((devices // 2, rows, width), jnp.bfloat16),
            pltpu.VMEM((4 * depth, half, width), jnp.bfloat16),
            pltpu.VMEM((2 * depth, half, width), jnp.bfloat16),
            pltpu.VMEM((2 * (depth - 1), half, width), jnp.bfloat16),
            pltpu.SemaphoreType.DMA((sends,)),
            pltpu.SemaphoreType.DMA((devices // 2, 2)),
            pltpu.SemaphoreType.DMA((4 * depth,)),
            pltpu.SemaphoreType.DMA((2 * depth,)),
            pltpu.SemaphoreType.DMA((2 * (depth - 1),)),
        ],
        compiler_params=pltpu.CompilerParams(
            collective_id=1, has_side_effects=True, vmem_limit_bytes=48 * 1024 * 1024
        ),
    )(parts)


def prelude_kernel(
    depth, keys_ref, w_o_ref, tags_ref, keys_out, w_out, tags_out, own_sem, send_sem, key_sem, w_sem, tag_sem
):
    x, core, z, y = place()
    half = w_o_ref.shape[0] // 2
    share = half * 3 // 8
    sibling = device(x, 1 - core, z, y)
    over_y = device(x, core, z, 1 - y)
    over_x = device(1 - x, core, z, y)
    over_z = [device(x, core, lax.rem(z + step, depth), y) for step in range(1, depth)]
    started = []

    def send(src, dst, recv_sem, target):
        copy = pltpu.make_async_remote_copy(
            src_ref=src,
            dst_ref=dst,
            send_sem=send_sem.at[len(started)],
            recv_sem=recv_sem,
            device_id=target,
            device_id_type=MESH,
        )
        copy.start()
        started.append(copy)

    def arrived(dst, recv_sem):
        pltpu.make_async_remote_copy(
            src_ref=dst,
            dst_ref=dst,
            send_sem=send_sem.at[0],
            recv_sem=recv_sem,
            device_id=sibling,
            device_id_type=MESH,
        ).wait_recv()

    def rows_of(on_core, piece):
        if isinstance(piece, int):
            return pl.ds(pl.multiple_of(on_core * half + 2 * share, 16), half - 2 * share)
        return pl.ds(pl.multiple_of(on_core * half + piece * share, 16), share)

    def w_send(block, on_core, piece, target, own=False):
        rows = rows_of(on_core, piece)
        send(
            w_o_ref.at[rows] if own else w_out.at[block, rows],
            w_out.at[block, rows],
            w_sem.at[block, on_core * 3 + piece],
            target,
        )

    def w_arrived(block, on_core, piece):
        arrived(w_out.at[block, rows_of(on_core, piece)], w_sem.at[block, on_core * 3 + piece])

    def slot(sx, sc, sz, sy):
        return (sx * 2 + sc) * (2 * depth) + sz * 2 + sy

    def tag_send(block, target, own=False):
        send(
            tags_ref if own else tags_out.at[block], tags_out.at[block], tag_sem.at[block], target
        )

    def tag_arrived(block):
        arrived(tags_out.at[block], tag_sem.at[block])

    greet([sibling, over_y, over_x] + over_z)
    me = z * 2 + y
    mine = slot(x, core, z, y)
    local = [
        pltpu.make_async_copy(keys_ref, keys_out.at[me], own_sem.at[0]),
        pltpu.make_async_copy(w_o_ref, w_out.at[me], own_sem.at[1]),
        pltpu.make_async_copy(tags_ref, tags_out.at[mine], own_sem.at[2]),
    ]
    for copy in local:
        copy.start()
    back = [lax.rem(z + depth - step, depth) for step in range(1, depth)]
    pieces = (x, 2)
    for target in over_z + [over_y]:
        send(keys_ref, keys_out.at[me], key_sem.at[me], target)
    for target in over_z + [over_y]:
        for piece in pieces:
            w_send(me, core, piece, target, True)
    for target in over_z + [over_y, over_x, sibling]:
        tag_send(mine, target, True)
    for sz in back:
        block = sz * 2 + y
        arrived(keys_out.at[block], key_sem.at[block])
        send(keys_out.at[block], keys_out.at[block], key_sem.at[block], over_y)
    for sz in back:
        block = sz * 2 + y
        for piece in pieces:
            w_arrived(block, core, piece)
            w_send(block, core, piece, over_y)
            if piece is x:
                w_send(block, core, piece, over_x)
            w_send(block, core, piece, sibling)
        tag = slot(x, core, sz, y)
        tag_arrived(tag)
        for target in (over_y, over_x, sibling):
            tag_send(tag, target)
    for sz in [z] + back:
        block = sz * 2 + 1 - y
        for piece in pieces:
            w_arrived(block, core, piece)
            if piece is x:
                w_send(block, core, piece, over_x)
            w_send(block, core, piece, sibling)
        tag = slot(x, core, sz, 1 - y)
        tag_arrived(tag)
        for target in (over_x, sibling):
            tag_send(tag, target)
    for sy in (y, 1 - y):
        for sz in [z] + back:
            block = sz * 2 + sy
            if not (sy is y and sz is z):
                w_arrived(block, core, 1 - x)
                w_send(block, core, 1 - x, sibling)
            tag = slot(1 - x, core, sz, sy)
            tag_arrived(tag)
            tag_send(tag, sibling)
    for sz in [z] + back:
        block = sz * 2 + 1 - y
        arrived(keys_out.at[block], key_sem.at[block])
        for sy in (y, 1 - y):
            block = sz * 2 + sy
            if not (sy is y and sz is z):
                for piece in (x, 1 - x, 2):
                    w_arrived(block, 1 - core, piece)
            for sx in (x, 1 - x):
                tag_arrived(slot(sx, 1 - core, sz, sy))
    for copy in local:
        copy.wait()
    for copy in started:
        copy.wait_send()


def prelude(keys, w_o, tags, devices, depth):
    key_sends = 2 * depth - 1
    w_sends = 2 * depth + 5 * (depth - 1) + 3 * depth + 2 * depth - 1
    tag_sends = depth + 2 + 3 * (depth - 1) + 2 * depth + 2 * depth
    return pl.pallas_call(
        lambda *refs: prelude_kernel(depth, *refs),
        name="prelude",
        out_shape=[
            jax.ShapeDtypeStruct((2 * depth,) + keys.shape, keys.dtype),
            jax.ShapeDtypeStruct((2 * depth,) + w_o.shape, w_o.dtype),
            jax.ShapeDtypeStruct((devices,) + tags.shape, tags.dtype),
        ],
        in_specs=[pl.BlockSpec(memory_space=pl.ANY)] * 3,
        out_specs=[pl.BlockSpec(memory_space=pl.ANY)] * 3,
        scratch_shapes=[
            pltpu.SemaphoreType.DMA((3,)),
            pltpu.SemaphoreType.DMA((key_sends + w_sends + tag_sends,)),
            pltpu.SemaphoreType.DMA((2 * depth,)),
            pltpu.SemaphoreType.DMA((2 * depth, 6)),
            pltpu.SemaphoreType.DMA((devices,)),
        ],
        compiler_params=pltpu.CompilerParams(collective_id=2, has_side_effects=True),
    )(keys, w_o, tags)


def dense_experts(normed, gate_up_w, down_w, experts, capacity, all_tags):
    devices = lax.axis_size("dp") * lax.axis_size("tensor")
    depth = lax.axis_size("tensor") // 2
    local_rows, model_width = normed.shape
    expert = (lax.axis_index("dp") * lax.axis_size("tensor") + lax.axis_index("tensor")) // 2
    share = lax.dynamic_index_in_dim(all_tags, expert, 1, keepdims=False)
    named = share != 0.0
    order = jnp.arange(local_rows, dtype=jnp.int32)
    upper = (order[:, None] <= order[None, :]).astype(jnp.bfloat16)
    rank = jnp.dot(named.astype(jnp.bfloat16), upper, preferred_element_type=jnp.float32) - 1.0
    slots = jnp.arange(capacity, dtype=jnp.int32)
    pick = named[:, None, :] & (rank.astype(jnp.int32)[:, None, :] == slots[None, :, None])
    slot_share = jnp.sum(jnp.where(pick, share[:, None, :], 0.0), axis=-1).reshape(-1, 1)
    pick = pick.astype(jnp.bfloat16)
    everyone = gather_rows(normed, devices, depth)
    rows = jnp.einsum("sct,std->scd", pick, everyone, preferred_element_type=jnp.float32)
    rows = rows.astype(jnp.bfloat16).reshape(devices * capacity, model_width)
    gate_up = jnp.dot(rows, gate_up_w, preferred_element_type=jnp.float32)
    half_units = down_w.shape[0]
    activated = (jax.nn.silu(gate_up[:, :half_units]) * gate_up[:, half_units:]).astype(
        jnp.bfloat16
    )
    scaled = (jnp.dot(activated, down_w, preferred_element_type=jnp.float32) * slot_share).astype(
        jnp.bfloat16
    )
    scaled = scaled.reshape(devices, capacity, model_width)
    parts = jnp.einsum("sct,scd->std", pick, scaled, preferred_element_type=jnp.float32)
    return reduce_rows(parts.astype(jnp.bfloat16), depth)


def on_device(
    hidden,
    query_nope,
    query_rope,
    segments,
    w_kva,
    w_kb,
    w_vb,
    w_o,
    route_ids,
    route_weights,
    w_in,
    w_down,
    page_table,
):
    groups = lax.axis_size("tensor")
    stream_groups = lax.axis_size("dp")
    member = lax.axis_index("tensor")
    tokens = hidden[0]
    local_rows = tokens.shape[0]
    model_width = tokens.shape[1]
    stream_len = segments.shape[1]
    n_heads, lat_width, head_width = w_kb.shape
    rope_width = w_kva.shape[1] - lat_width
    top_count = route_ids.shape[2]
    scale = float(head_width + rope_width) ** (-0.5)
    kv_proj = jnp.dot(tokens, w_kva, preferred_element_type=jnp.float32)
    latent = rms_rows(kv_proj[:, :lat_width]).astype(jnp.bfloat16)
    first_row = member * local_rows
    positions = first_row + jnp.arange(local_rows, dtype=jnp.int32)
    key_rope = rotate(kv_proj[:, lat_width:], positions).astype(jnp.bfloat16)
    query_rot = rotate(
        query_rope[0].astype(jnp.float32).reshape(local_rows, n_heads, rope_width),
        positions[:, None],
    ).astype(jnp.bfloat16)
    query_lat = jnp.einsum(
        "thd,hld->thl",
        query_nope[0].reshape(local_rows, n_heads, head_width),
        w_kb,
        preferred_element_type=jnp.float32,
    ).astype(jnp.bfloat16)
    seg_all = segments[0]
    query_seg = lax.dynamic_slice_in_dim(seg_all, first_row, local_rows, 0)
    key_low = jnp.sum((seg_all < query_seg[0]).astype(jnp.int32))
    key_high = first_row + local_rows
    queries = (query_lat, query_rot, query_seg, positions, scale)
    start_state = (
        jnp.full((local_rows, n_heads), masked_score, jnp.float32),
        jnp.zeros((local_rows, n_heads), jnp.float32),
        jnp.zeros((local_rows, n_heads, lat_width), jnp.float32),
    )
    pages_dev = local_rows // PAGE
    page_row = page_table[0]
    slot_ids = member * pages_dev + jnp.arange(pages_dev, dtype=jnp.int32)
    page_of = jnp.sum(
        jnp.where(
            page_row[None, :] == slot_ids[:, None],
            jnp.arange(page_row.shape[0], dtype=jnp.int32)[None, :],
            0,
        ),
        axis=1,
    )
    page_rows = page_of[:, None] * PAGE + jnp.arange(PAGE, dtype=jnp.int32)[None, :]
    experts = stream_groups * groups // 2
    capacity = max(2, min(local_rows, local_rows * top_count * 4 // (3 * experts)))
    dense = stream_groups * groups * local_rows <= 4 * experts * capacity
    my_keys = jnp.concatenate([latent, key_rope], axis=1)
    if dense:
        one_hot = route_ids[0][None] == jnp.arange(experts, dtype=jnp.int32)[:, None, None]
        tags = jnp.sum(jnp.where(one_hot, route_weights[0][None], 0.0), axis=2)
        all_keys, all_w_o, all_tags = prelude(
            my_keys, w_o, tags, stream_groups * groups, groups // 2
        )
        all_keys = all_keys.reshape(stream_len, -1)
        all_w_o = all_w_o.reshape(-1, model_width)
    else:
        all_keys = lax.all_gather(my_keys, "tensor", axis=0, tiled=True)
        all_w_o = lax.all_gather(w_o, "tensor", axis=0, tiled=True)
    all_latent, all_rope = all_keys[:, :lat_width], all_keys[:, lat_width:]
    key_block = min(512, stream_len)
    block_first = key_low // key_block
    block_end = (key_high + key_block - 1) // key_block

    def key_step(block_no, carry_in):
        key_first = block_no * key_block
        keys_lat = lax.dynamic_slice_in_dim(all_latent, key_first, key_block, 0)
        keys_rot = lax.dynamic_slice_in_dim(all_rope, key_first, key_block, 0)
        keys_seg = lax.dynamic_slice_in_dim(seg_all, key_first, key_block, 0)
        return attend(carry_in, queries, keys_lat, keys_rot, keys_seg, key_first)

    final_state = lax.fori_loop(block_first, block_end, key_step, start_state)
    pool_lat = all_latent[page_rows]
    pool_rot = all_rope[page_rows]
    mixed_lat = (final_state[2] / final_state[1][..., None]).astype(jnp.bfloat16)
    heads_out = (
        jnp.einsum("thl,hld->thd", mixed_lat, w_vb, preferred_element_type=jnp.float32)
        .astype(jnp.bfloat16)
        .reshape(local_rows, n_heads * head_width)
    )
    attn_out = jnp.dot(heads_out, all_w_o, preferred_element_type=jnp.float32)
    resid = (tokens.astype(jnp.float32) + attn_out).astype(jnp.bfloat16)
    normed = rms_rows(resid.astype(jnp.float32)).astype(jnp.bfloat16)
    if dense:
        moe_out = dense_experts(
            normed,
            w_in[0],
            w_down[0],
            experts,
            capacity,
            all_tags,
        )
        layer_out = (resid.astype(jnp.float32) + moe_out).astype(jnp.bfloat16)
        return (layer_out[None], pool_lat[None], pool_rot[None])
    expert_ids = route_ids[0].reshape(-1)
    assign_total = local_rows * top_count
    one_hot = (expert_ids[:, None] == jnp.arange(experts, dtype=jnp.int32)[None, :]).astype(
        jnp.int32
    )
    slot_in = jnp.sum((jnp.cumsum(one_hot, axis=0) - 1) * one_hot, axis=1)
    buffer_pos = expert_ids * capacity + slot_in
    source = (
        jnp.full((experts * capacity,), assign_total, jnp.int32)
        .at[buffer_pos]
        .set(jnp.arange(assign_total, dtype=jnp.int32))
    )
    padded = jnp.concatenate([normed, jnp.zeros((1, model_width), jnp.bfloat16)], axis=0)
    gathered_rows = padded[source // top_count]
    sending = gathered_rows.reshape(experts, 1, capacity, model_width)
    sending = jnp.broadcast_to(sending, (experts, 2, capacity, model_width)).reshape(
        2 * experts, capacity, model_width
    )
    returned = lax.all_to_all(
        expert_rows(
            lax.all_to_all(sending, ("dp", "tensor"), split_axis=0, concat_axis=0, tiled=True),
            w_in[0],
            w_down[0],
        ),
        ("dp", "tensor"),
        split_axis=0,
        concat_axis=0,
        tiled=True,
    )
    pairs = returned.reshape(experts, 2, capacity, model_width)
    merged = (pairs[:, 0].astype(jnp.float32) + pairs[:, 1].astype(jnp.float32)).reshape(
        experts * capacity, model_width
    )
    picked = merged[buffer_pos]
    weight_flat = route_weights[0].reshape(-1)
    moe_out = jnp.sum(
        (picked * weight_flat[:, None]).reshape(local_rows, top_count, model_width), axis=1
    )
    layer_out = (resid.astype(jnp.float32) + moe_out).astype(jnp.bfloat16)
    return (layer_out[None], pool_lat[None], pool_rot[None])


def solution(mesh):
    return jax.shard_map(
        on_device,
        mesh=mesh,
        in_specs=(
            P("dp", "tensor", None),
            P("dp", "tensor", None),
            P("dp", "tensor", None),
            P("dp", None),
            P(),
            P(),
            P(),
            P("tensor", None),
            P("dp", "tensor", None),
            P("dp", "tensor", None),
            P(("dp", "tensor"), None, None),
            P(("dp", "tensor"), None, None),
            P("dp", None),
        ),
        out_specs=(
            P("dp", "tensor", None),
            P("dp", "tensor", None, None),
            P("dp", "tensor", None, None),
        ),
        check_vma=False,
    )
```

```python
import jax
import jax.numpy as jnp
from jax import lax
from jax.experimental import pallas as pl
from jax.experimental.pallas import tpu as pltpu
from jax.sharding import PartitionSpec as P

MESH = pl.DeviceIdType.MESH

PAGE = 128


eps_norm = 1e-06
masked_score = -1e30


def rms_rows(values):
    return values * lax.rsqrt(jnp.mean(values * values, axis=-1, keepdims=True) + eps_norm)


def rotate(values, positions):
    width = values.shape[-1]
    half_width = width // 2
    freqs = 10000.0 ** (-jnp.arange(half_width, dtype=jnp.float32) * 2.0 / width)
    angles = positions[..., None].astype(jnp.float32) * freqs
    cosine = jnp.cos(angles)
    sine = jnp.sin(angles)
    first_half = values[..., :half_width]
    second_half = values[..., half_width:]
    return jnp.concatenate(
        [first_half * cosine - second_half * sine, first_half * sine + second_half * cosine],
        axis=-1,
    )


def attend(carry_in, queries, keys_lat, keys_rot, keys_seg, key_first):
    peak, row_sum, numerator = carry_in
    query_lat, query_rot, query_seg, positions, scale = queries
    scores = jnp.einsum("qhl,kl->qhk", query_lat, keys_lat, preferred_element_type=jnp.float32)
    scores = (
        scores + jnp.einsum("qhr,kr->qhk", query_rot, keys_rot, preferred_element_type=jnp.float32)
    ) * scale
    key_pos = key_first + jnp.arange(keys_lat.shape[0], dtype=jnp.int32)
    allowed = (query_seg[:, None] == keys_seg[None, :]) & (key_pos[None, :] <= positions[:, None])
    scores = jnp.where(allowed[:, None, :], scores, masked_score)
    new_peak = jnp.maximum(peak, jnp.max(scores, axis=-1))
    shrink = jnp.exp(peak - new_peak)
    expo = jnp.exp(scores - new_peak[..., None])
    row_sum = row_sum * shrink + jnp.sum(expo, axis=-1)
    numerator = numerator * shrink[..., None] + jnp.einsum(
        "qhk,kl->qhl", expo.astype(jnp.bfloat16), keys_lat, preferred_element_type=jnp.float32
    )
    return (new_peak, row_sum, numerator)


def expert_rows(received, gate_up_w, down_w):
    model_width = received.shape[-1]
    flat_rows = received.reshape(-1, model_width)
    gate_up = jnp.dot(flat_rows, gate_up_w, preferred_element_type=jnp.float32)
    half_units = down_w.shape[0]
    activated = (jax.nn.silu(gate_up[:, :half_units]) * gate_up[:, half_units:]).astype(
        jnp.bfloat16
    )
    return (
        jnp.dot(activated, down_w, preferred_element_type=jnp.float32)
        .astype(jnp.bfloat16)
        .reshape(received.shape)
    )


def place():
    dp = lax.axis_index("dp")
    member = lax.axis_index("tensor")
    return dp // 2, dp % 2, member // 2, member % 2


def device(x, core, z, y):
    return {"dp": x * 2 + core, "tensor": z * 2 + y}


def greet(partners):
    barrier = pltpu.get_barrier_semaphore()
    for partner in partners:
        pl.semaphore_signal(barrier, inc=1, device_id=partner, device_id_type=MESH)
    pl.semaphore_wait(barrier, len(partners))


def by_distance(z, depth):
    tables = [
        sorted([other for other in range(depth) if other != here], key=lambda other: abs(other - here))
        for here in range(depth)
    ]
    return [
        sum(jnp.where(z == here, tables[here][number], 0) for here in range(depth))
        for number in range(depth - 1)
    ]


def gather_kernel(depth, rows_ref, out_ref, own_sem, send_sem, recv_sem):
    x, core, z, y = place()
    half = rows_ref.shape[0] // 2
    sibling = device(x, 1 - core, z, y)
    over_y = device(x, core, z, 1 - y)
    over_x = device(1 - x, core, z, y)
    others = by_distance(z, depth)
    up = device(x, core, jnp.minimum(z + 1, depth - 1), y)
    down = device(x, core, jnp.maximum(z - 1, 0), y)
    started = []

    def slot(sx, sc, sz, sy):
        return (sx * 2 + sc) * (2 * depth) + sz * 2 + sy

    def send(block, part, target, own=False, when=None):
        span = pl.ds(part * half, half)
        copy = pltpu.make_async_remote_copy(
            src_ref=rows_ref.at[span] if own else out_ref.at[block, span],
            dst_ref=out_ref.at[block, span],
            send_sem=send_sem.at[len(started)],
            recv_sem=recv_sem.at[block, part],
            device_id=target,
            device_id_type=MESH,
        )
        if when is None:
            copy.start()
        else:
            pl.when(when)(copy.start)
        started.append((copy, when))

    def arrived(block, part):
        span = pl.ds(part * half, half)
        pltpu.make_async_remote_copy(
            src_ref=out_ref.at[block, span],
            dst_ref=out_ref.at[block, span],
            send_sem=send_sem.at[0],
            recv_sem=recv_sem.at[block, part],
            device_id=sibling,
            device_id_type=MESH,
        ).wait_recv()

    greet([sibling, over_y, over_x] + [device(x, core, other, y) for other in others])
    mine = slot(x, core, z, y)
    own = pltpu.make_async_copy(rows_ref, out_ref.at[mine], own_sem)
    own.start()
    near = (over_y, over_x)
    for part in range(2):
        send(mine, part, up, True, z < depth - 1)
        send(mine, part, down, True, z > 0)
    for part in range(2):
        send(mine, part, near[part], True)
        send(mine, part, near[1 - part], True)
        send(mine, part, sibling, True)
    for sz in others:
        for part in range(2):
            block = slot(x, core, sz, y)
            arrived(block, part)
            send(block, part, up, False, (sz < z) & (z < depth - 1))
            send(block, part, down, False, (sz > z) & (z > 0))
            send(block, part, near[part])
            send(block, part, near[1 - part])
            send(block, part, sibling)
    for sz in [z] + others:
        for part in range(2):
            block = slot(x, core, sz, 1 - y) if part == 0 else slot(1 - x, core, sz, y)
            arrived(block, part)
            send(block, part, near[1 - part])
            send(block, part, sibling)
    for far in range(2):
        for sz in [z] + others:
            for part in range(2):
                if part == 0:
                    block = slot(1 - x, core, sz, (y + far) % 2)
                else:
                    block = slot((x + far) % 2, core, sz, 1 - y)
                arrived(block, part)
                send(block, part, sibling)
    for sz in [z] + others:
        for sx in range(2):
            for sy in range(2):
                for part in range(2):
                    arrived(slot(sx, 1 - core, sz, sy), part)
    own.wait()
    for copy, when in started:
        if when is None:
            copy.wait_send()
        else:
            pl.when(when)(copy.wait_send)


def gather_rows(rows, devices, depth):
    sends = 2 * (2 * depth + depth + 2 * depth + 4 * depth)
    return pl.pallas_call(
        lambda *refs: gather_kernel(depth, *refs),
        name="gather_rows",
        out_shape=jax.ShapeDtypeStruct((devices,) + rows.shape, rows.dtype),
        in_specs=[pl.BlockSpec(memory_space=pl.ANY)],
        out_specs=pl.BlockSpec(memory_space=pl.ANY),
        scratch_shapes=[
            pltpu.SemaphoreType.DMA,
            pltpu.SemaphoreType.DMA((sends,)),
            pltpu.SemaphoreType.DMA((devices, 2)),
        ],
        compiler_params=pltpu.CompilerParams(collective_id=0, has_side_effects=True),
    )(rows)


def reduce_kernel(
    depth, slots_ref, pick_ref, out_ref, outgoing, first, second, third, fourth, send_sem, sem1, sem2, sem3, sem4
):
    x, core, z, y = place()
    half = out_ref.shape[0] // 2
    chunk = 512
    sibling = device(x, 1 - core, z, y)
    over_y = device(x, core, z, 1 - y)
    over_x = device(1 - x, core, z, y)
    others = [lax.rem(z + step, depth) for step in range(1, depth)]
    greet([sibling, over_y, over_x] + [device(x, core, other, y) for other in others])
    started = []

    def send(src, dst, recv_sem, target):
        copy = pltpu.make_async_remote_copy(
            src_ref=src,
            dst_ref=dst,
            send_sem=send_sem.at[len(started)],
            recv_sem=recv_sem,
            device_id=target,
            device_id_type=MESH,
        )
        copy.start()
        started.append(copy)

    def arrived(dst, recv_sem):
        pltpu.make_async_remote_copy(
            src_ref=dst,
            dst_ref=dst,
            send_sem=send_sem.at[0],
            recv_sem=recv_sem,
            device_id=sibling,
            device_id_type=MESH,
        ).wait_recv()

    def slot(dx, dc, dz, dy):
        return (dx * 2 + dc) * (2 * depth) + dz * 2 + dy

    def plane(dx, dz, dy):
        return (dx * 2 + dy) * depth + dz

    def span(part):
        return pl.ds(part * half, half)

    def add_into(target, block, part, sources):
        picked = pick_ref[block, span(part), :]

        def body(step, carry):
            columns = pl.ds(pl.multiple_of(step * chunk, chunk), chunk)
            total = jnp.dot(picked, slots_ref[block, :, columns], preferred_element_type=jnp.float32)
            for ref, index, whole in sources:
                value = ref[index, span(part), columns] if whole else ref[index, :, columns]
                total = total + value.astype(jnp.float32)
            if target is None:
                out_ref[span(part), columns] = total
            elif target[2]:
                target[0][target[1], span(part), columns] = total.astype(jnp.bfloat16)
            else:
                target[0][target[1], :, columns] = total.astype(jnp.bfloat16)
            return carry

        lax.fori_loop(0, out_ref.shape[1] // chunk, body, 0)

    def inner(part, near, dz):
        return (near * depth + dz) * 2 + part

    steps = [lax.rem(z + step, depth) for step in list(range(1, depth)) + [0]]

    def dest(part, far_first, far_second):
        if part == 0:
            return (x + far_first) % 2, (y + far_second) % 2
        return (x + far_second) % 2, (y + far_first) % 2

    order = [(1, 1), (1, 0), (0, 1), (0, 0)]
    for far_first, far_second in order:
        for dz in steps:
            for part in range(2):
                dx, dy = dest(part, far_first, far_second)
                index = plane(dx, dz, dy)
                add_into((outgoing, index, True), slot(dx, 1 - core, dz, dy), part, [])
                send(
                    outgoing.at[index, span(part)],
                    first.at[index, span(part)],
                    sem1.at[index, part],
                    sibling,
                )
    for far_second in (1, 0):
        for dz in steps:
            for part in range(2):
                dx, dy = dest(part, 1, far_second)
                index = plane(dx, dz, dy)
                arrived(first.at[index, span(part)], sem1.at[index, part])
                add_into(
                    (first, index, True),
                    slot(dx, core, dz, dy),
                    part,
                    [(first, index, True)],
                )
                there = inner(part, far_second, dz)
                send(
                    first.at[index, span(part)],
                    second.at[there],
                    sem2.at[there],
                    over_x if part == 0 else over_y,
                )
    for dz in steps:
        for part in range(2):
            dx, dy = dest(part, 0, 1)
            index = plane(dx, dz, dy)
            there = inner(part, 1, dz)
            arrived(first.at[index, span(part)], sem1.at[index, part])
            arrived(second.at[there], sem2.at[there])
            add_into(
                (second, there, False),
                slot(dx, core, dz, dy),
                part,
                [(first, index, True), (second, there, False)],
            )
            last = dz * 2 + part
            send(
                second.at[there],
                third.at[last],
                sem3.at[last],
                over_y if part == 0 else over_x,
            )
    for number, dz in enumerate(steps):
        for part in range(2):
            index = plane(x, dz, y)
            there = inner(part, 0, dz)
            last = dz * 2 + part
            arrived(first.at[index, span(part)], sem1.at[index, part])
            arrived(second.at[there], sem2.at[there])
            arrived(third.at[last], sem3.at[last])
            block = slot(x, core, dz, y)
            sources = [
                (first, index, True),
                (second, there, False),
                (third, last, False),
            ]
            if number < depth - 1:
                add_into((third, last, False), block, part, sources)
                end = number * 2 + part
                send(third.at[last], fourth.at[end], sem4.at[end], device(x, core, dz, y))
            else:
                for other in range(depth - 1):
                    end = other * 2 + part
                    arrived(fourth.at[end], sem4.at[end])
                    sources.append((fourth, end, False))
                add_into(None, block, part, sources)
    for copy in started:
        copy.wait_send()


def reduce_rows(slots, pick, depth):
    devices, rows, _ = pick.shape
    width = slots.shape[2]
    half = rows // 2
    sends = 8 * depth + 4 * depth + 2 * depth + 2 * (depth - 1)
    return pl.pallas_call(
        lambda *refs: reduce_kernel(depth, *refs),
        name="reduce_rows",
        out_shape=jax.ShapeDtypeStruct((rows, width), jnp.float32),
        in_specs=[pl.BlockSpec(memory_space=pltpu.VMEM)] * 2,
        out_specs=pl.BlockSpec(memory_space=pltpu.VMEM),
        scratch_shapes=[
            pltpu.VMEM((devices // 2, rows, width), jnp.bfloat16),
            pltpu.VMEM((devices // 2, rows, width), jnp.bfloat16),
            pltpu.VMEM((4 * depth, half, width), jnp.bfloat16),
            pltpu.VMEM((2 * depth, half, width), jnp.bfloat16),
            pltpu.VMEM((2 * (depth - 1), half, width), jnp.bfloat16),
            pltpu.SemaphoreType.DMA((sends,)),
            pltpu.SemaphoreType.DMA((devices // 2, 2)),
            pltpu.SemaphoreType.DMA((4 * depth,)),
            pltpu.SemaphoreType.DMA((2 * depth,)),
            pltpu.SemaphoreType.DMA((2 * (depth - 1),)),
        ],
        compiler_params=pltpu.CompilerParams(
            collective_id=1, has_side_effects=True, vmem_limit_bytes=48 * 1024 * 1024
        ),
    )(slots, pick)


def prelude_kernel(
    depth, keys_ref, tags_ref, keys_out, tags_out, own_sem, send_sem, key_sem, tag_sem
):
    x, core, z, y = place()
    sibling = device(x, 1 - core, z, y)
    over_y = device(x, core, z, 1 - y)
    over_x = device(1 - x, core, z, y)
    over_z = [device(x, core, lax.rem(z + step, depth), y) for step in range(1, depth)]
    started = []

    def send(src, dst, recv_sem, target):
        copy = pltpu.make_async_remote_copy(
            src_ref=src,
            dst_ref=dst,
            send_sem=send_sem.at[len(started)],
            recv_sem=recv_sem,
            device_id=target,
            device_id_type=MESH,
        )
        copy.start()
        started.append(copy)

    def arrived(dst, recv_sem):
        pltpu.make_async_remote_copy(
            src_ref=dst,
            dst_ref=dst,
            send_sem=send_sem.at[0],
            recv_sem=recv_sem,
            device_id=sibling,
            device_id_type=MESH,
        ).wait_recv()

    def slot(sx, sc, sz, sy):
        return (sx * 2 + sc) * (2 * depth) + sz * 2 + sy

    def tag_send(block, target, own=False):
        send(
            tags_ref if own else tags_out.at[block], tags_out.at[block], tag_sem.at[block], target
        )

    def tag_arrived(block):
        arrived(tags_out.at[block], tag_sem.at[block])

    greet([sibling, over_y, over_x] + over_z)
    me = z * 2 + y
    mine = slot(x, core, z, y)
    local = [
        pltpu.make_async_copy(keys_ref, keys_out.at[me], own_sem.at[0]),
        pltpu.make_async_copy(tags_ref, tags_out.at[mine], own_sem.at[1]),
    ]
    for copy in local:
        copy.start()
    back = [lax.rem(z + depth - step, depth) for step in range(1, depth)]
    for target in over_z + [over_y]:
        send(keys_ref, keys_out.at[me], key_sem.at[me], target)
    for target in over_z + [over_y, over_x, sibling]:
        tag_send(mine, target, True)
    for sz in back:
        block = sz * 2 + y
        arrived(keys_out.at[block], key_sem.at[block])
        send(keys_out.at[block], keys_out.at[block], key_sem.at[block], over_y)
    for sz in back:
        tag = slot(x, core, sz, y)
        tag_arrived(tag)
        for target in (over_y, over_x, sibling):
            tag_send(tag, target)
    for sz in [z] + back:
        tag = slot(x, core, sz, 1 - y)
        tag_arrived(tag)
        for target in (over_x, sibling):
            tag_send(tag, target)
    for sy in (y, 1 - y):
        for sz in [z] + back:
            tag = slot(1 - x, core, sz, sy)
            tag_arrived(tag)
            tag_send(tag, sibling)
    for sz in [z] + back:
        block = sz * 2 + 1 - y
        arrived(keys_out.at[block], key_sem.at[block])
        for sy in (y, 1 - y):
            for sx in (x, 1 - x):
                tag_arrived(slot(sx, 1 - core, sz, sy))
    for copy in local:
        copy.wait()
    for copy in started:
        copy.wait_send()


def prelude(keys, tags, devices, depth):
    key_sends = 2 * depth - 1
    tag_sends = depth + 2 + 3 * (depth - 1) + 2 * depth + 2 * depth
    return pl.pallas_call(
        lambda *refs: prelude_kernel(depth, *refs),
        name="prelude",
        out_shape=[
            jax.ShapeDtypeStruct((2 * depth,) + keys.shape, keys.dtype),
            jax.ShapeDtypeStruct((devices,) + tags.shape, tags.dtype),
        ],
        in_specs=[pl.BlockSpec(memory_space=pl.ANY)] * 2,
        out_specs=[pl.BlockSpec(memory_space=pl.ANY)] * 2,
        scratch_shapes=[
            pltpu.SemaphoreType.DMA((2,)),
            pltpu.SemaphoreType.DMA((key_sends + tag_sends,)),
            pltpu.SemaphoreType.DMA((2 * depth,)),
            pltpu.SemaphoreType.DMA((devices,)),
        ],
        compiler_params=pltpu.CompilerParams(collective_id=2, has_side_effects=True),
    )(keys, tags)


def dense_experts(normed, gate_up_w, down_w, experts, capacity, all_tags):
    devices = lax.axis_size("dp") * lax.axis_size("tensor")
    depth = lax.axis_size("tensor") // 2
    local_rows, model_width = normed.shape
    expert = (lax.axis_index("dp") * lax.axis_size("tensor") + lax.axis_index("tensor")) // 2
    share = lax.dynamic_index_in_dim(all_tags, expert, 1, keepdims=False)
    named = share != 0.0
    order = jnp.arange(local_rows, dtype=jnp.int32)
    upper = (order[:, None] <= order[None, :]).astype(jnp.bfloat16)
    rank = jnp.dot(named.astype(jnp.bfloat16), upper, preferred_element_type=jnp.float32) - 1.0
    slots = jnp.arange(capacity, dtype=jnp.int32)
    pick = named[:, None, :] & (rank.astype(jnp.int32)[:, None, :] == slots[None, :, None])
    slot_share = jnp.sum(jnp.where(pick, share[:, None, :], 0.0), axis=-1).reshape(-1, 1)
    pick = pick.astype(jnp.bfloat16)
    everyone = gather_rows(normed, devices, depth)
    rows = jnp.einsum("sct,std->scd", pick, everyone, preferred_element_type=jnp.float32)
    rows = rows.astype(jnp.bfloat16).reshape(devices * capacity, model_width)
    gate_up = jnp.dot(rows, gate_up_w, preferred_element_type=jnp.float32)
    half_units = down_w.shape[0]
    activated = (jax.nn.silu(gate_up[:, :half_units]) * gate_up[:, half_units:]).astype(
        jnp.bfloat16
    )
    scaled = (jnp.dot(activated, down_w, preferred_element_type=jnp.float32) * slot_share).astype(
        jnp.bfloat16
    )
    scaled = scaled.reshape(devices, capacity, model_width)
    return reduce_rows(scaled, jnp.swapaxes(pick, 1, 2), depth)


def on_device(
    hidden,
    query_nope,
    query_rope,
    segments,
    w_kva,
    w_kb,
    w_vb,
    w_o,
    route_ids,
    route_weights,
    w_in,
    w_down,
    page_table,
):
    groups = lax.axis_size("tensor")
    stream_groups = lax.axis_size("dp")
    member = lax.axis_index("tensor")
    tokens = hidden[0]
    local_rows = tokens.shape[0]
    model_width = tokens.shape[1]
    stream_len = segments.shape[1]
    n_heads, lat_width, head_width = w_kb.shape
    rope_width = w_kva.shape[1] - lat_width
    top_count = route_ids.shape[2]
    scale = float(head_width + rope_width) ** (-0.5)
    kv_proj = jnp.dot(tokens, w_kva, preferred_element_type=jnp.float32)
    latent = rms_rows(kv_proj[:, :lat_width]).astype(jnp.bfloat16)
    first_row = member * local_rows
    positions = first_row + jnp.arange(local_rows, dtype=jnp.int32)
    key_rope = rotate(kv_proj[:, lat_width:], positions).astype(jnp.bfloat16)
    query_rot = rotate(
        query_rope[0].astype(jnp.float32).reshape(local_rows, n_heads, rope_width),
        positions[:, None],
    ).astype(jnp.bfloat16)
    query_lat = jnp.einsum(
        "thd,hld->thl",
        query_nope[0].reshape(local_rows, n_heads, head_width),
        w_kb,
        preferred_element_type=jnp.float32,
    ).astype(jnp.bfloat16)
    seg_all = segments[0]
    query_seg = lax.dynamic_slice_in_dim(seg_all, first_row, local_rows, 0)
    key_low = jnp.sum((seg_all < query_seg[0]).astype(jnp.int32))
    key_high = first_row + local_rows
    queries = (query_lat, query_rot, query_seg, positions, scale)
    start_state = (
        jnp.full((local_rows, n_heads), masked_score, jnp.float32),
        jnp.zeros((local_rows, n_heads), jnp.float32),
        jnp.zeros((local_rows, n_heads, lat_width), jnp.float32),
    )
    pages_dev = local_rows // PAGE
    page_row = page_table[0]
    slot_ids = member * pages_dev + jnp.arange(pages_dev, dtype=jnp.int32)
    page_of = jnp.sum(
        jnp.where(
            page_row[None, :] == slot_ids[:, None],
            jnp.arange(page_row.shape[0], dtype=jnp.int32)[None, :],
            0,
        ),
        axis=1,
    )
    page_rows = page_of[:, None] * PAGE + jnp.arange(PAGE, dtype=jnp.int32)[None, :]
    experts = stream_groups * groups // 2
    capacity = max(2, min(local_rows, local_rows * top_count * 4 // (3 * experts)))
    dense = stream_groups * groups * local_rows <= 4 * experts * capacity
    my_keys = jnp.concatenate([latent, key_rope], axis=1)
    if dense:
        one_hot = route_ids[0][None] == jnp.arange(experts, dtype=jnp.int32)[:, None, None]
        tags = jnp.sum(jnp.where(one_hot, route_weights[0][None], 0.0), axis=2)
        all_keys, all_tags = prelude(my_keys, tags, stream_groups * groups, groups // 2)
        all_keys = all_keys.reshape(stream_len, -1)
    else:
        all_keys = lax.all_gather(my_keys, "tensor", axis=0, tiled=True)
    core = lax.axis_index("dp") % 2
    half_width = model_width // 2
    my_columns = lax.all_gather(
        lax.dynamic_slice_in_dim(w_o, core * half_width, half_width, 1),
        "tensor",
        axis=0,
        tiled=True,
    )
    all_latent, all_rope = all_keys[:, :lat_width], all_keys[:, lat_width:]
    key_block = min(512, stream_len)
    block_first = key_low // key_block
    block_end = (key_high + key_block - 1) // key_block

    def key_step(block_no, carry_in):
        key_first = block_no * key_block
        keys_lat = lax.dynamic_slice_in_dim(all_latent, key_first, key_block, 0)
        keys_rot = lax.dynamic_slice_in_dim(all_rope, key_first, key_block, 0)
        keys_seg = lax.dynamic_slice_in_dim(seg_all, key_first, key_block, 0)
        return attend(carry_in, queries, keys_lat, keys_rot, keys_seg, key_first)

    final_state = lax.fori_loop(block_first, block_end, key_step, start_state)
    pool_lat = all_latent[page_rows]
    pool_rot = all_rope[page_rows]
    mixed_lat = (final_state[2] / final_state[1][..., None]).astype(jnp.bfloat16)
    heads_out = (
        jnp.einsum("thl,hld->thd", mixed_lat, w_vb, preferred_element_type=jnp.float32)
        .astype(jnp.bfloat16)
        .reshape(local_rows, n_heads * head_width)
    )
    my_columns, heads_out = lax.optimization_barrier((my_columns, heads_out))
    its_columns = lax.ppermute(
        my_columns, "dp", [(number, number ^ 1) for number in range(stream_groups)]
    )
    my_out = jnp.dot(heads_out, my_columns, preferred_element_type=jnp.float32)
    its_out = jnp.dot(heads_out, its_columns, preferred_element_type=jnp.float32)
    attn_out = jnp.where(
        core == 0,
        jnp.concatenate([my_out, its_out], axis=1),
        jnp.concatenate([its_out, my_out], axis=1),
    )
    resid = (tokens.astype(jnp.float32) + attn_out).astype(jnp.bfloat16)
    normed = rms_rows(resid.astype(jnp.float32)).astype(jnp.bfloat16)
    if dense:
        moe_out = dense_experts(
            normed,
            w_in[0],
            w_down[0],
            experts,
            capacity,
            all_tags,
        )
        layer_out = (resid.astype(jnp.float32) + moe_out).astype(jnp.bfloat16)
        return (layer_out[None], pool_lat[None], pool_rot[None])
    expert_ids = route_ids[0].reshape(-1)
    assign_total = local_rows * top_count
    one_hot = (expert_ids[:, None] == jnp.arange(experts, dtype=jnp.int32)[None, :]).astype(
        jnp.int32
    )
    slot_in = jnp.sum((jnp.cumsum(one_hot, axis=0) - 1) * one_hot, axis=1)
    buffer_pos = expert_ids * capacity + slot_in
    source = (
        jnp.full((experts * capacity,), assign_total, jnp.int32)
        .at[buffer_pos]
        .set(jnp.arange(assign_total, dtype=jnp.int32))
    )
    padded = jnp.concatenate([normed, jnp.zeros((1, model_width), jnp.bfloat16)], axis=0)
    gathered_rows = padded[source // top_count]
    sending = gathered_rows.reshape(experts, 1, capacity, model_width)
    sending = jnp.broadcast_to(sending, (experts, 2, capacity, model_width)).reshape(
        2 * experts, capacity, model_width
    )
    returned = lax.all_to_all(
        expert_rows(
            lax.all_to_all(sending, ("dp", "tensor"), split_axis=0, concat_axis=0, tiled=True),
            w_in[0],
            w_down[0],
        ),
        ("dp", "tensor"),
        split_axis=0,
        concat_axis=0,
        tiled=True,
    )
    pairs = returned.reshape(experts, 2, capacity, model_width)
    merged = (pairs[:, 0].astype(jnp.float32) + pairs[:, 1].astype(jnp.float32)).reshape(
        experts * capacity, model_width
    )
    picked = merged[buffer_pos]
    weight_flat = route_weights[0].reshape(-1)
    moe_out = jnp.sum(
        (picked * weight_flat[:, None]).reshape(local_rows, top_count, model_width), axis=1
    )
    layer_out = (resid.astype(jnp.float32) + moe_out).astype(jnp.bfloat16)
    return (layer_out[None], pool_lat[None], pool_rot[None])


def solution(mesh):
    return jax.shard_map(
        on_device,
        mesh=mesh,
        in_specs=(
            P("dp", "tensor", None),
            P("dp", "tensor", None),
            P("dp", "tensor", None),
            P("dp", None),
            P(),
            P(),
            P(),
            P("tensor", None),
            P("dp", "tensor", None),
            P("dp", "tensor", None),
            P(("dp", "tensor"), None, None),
            P(("dp", "tensor"), None, None),
            P("dp", None),
        ),
        out_specs=(
            P("dp", "tensor", None),
            P("dp", "tensor", None, None),
            P("dp", "tensor", None, None),
        ),
        check_vma=False,
    )
```
